256 devices in a mesh: outer: 2 (over core), inner: 32 (over z, x), head: 4 (over y).
Axes of the slice: x: 4, y: 4, z: 8, core: 2. Of those that a mesh axis runs over, the one named last changes fastest.
Arguments:
- queries: bfloat16 [512, 64, 128], P('inner', 'head'), may hold values from -20 to 20
- keys: bfloat16 [131072, 8, 128], P(('outer', 'inner'), 'head'), may hold values from -15 to 15
- values: bfloat16 [131072, 8, 128], P(('outer', 'inner'), 'head'), may hold values from -6 to 6
- doc_lengths: int32 [32], replicated, may hold values from 1 to 256, 1024 in all
Outputs:
- attended: bfloat16 [512, 64, 128], P('inner', 'head')
The draws below stay inside these ranges and needn't reach their ends.
All inputs are finite; a program needn't handle non-finite values.
Results may differ from the reference program's by a relative error of at most 0.003.
Values may be sent and summed in bfloat16 or wider, within the bound.
No kernel may reach another device: no remote copies, remote signals or barrier semaphores. Data moves between devices by JAX's collectives and lax.ppermute only.
A program may use at most 256 MiB of HBM per device.

```python
import math
import jax
import jax.numpy as jnp
import numpy as np
from jax import lax

HEADS = 64
KV_HEADS = 8
DH = 128
KV_DEV = 2048
QT = 8
BLOCK = 128
DOCS = 32
OUTER_GROUPS = 2
CYCLE = 32
SEQ = 131072
NBLK = 1024
MOST_BLK = 256
QROWS = 512


def draw_together(key):
    base = jax.random.fold_in(key, 7)
    first = jax.random.fold_in(base, 1)
    second = jax.random.fold_in(base, 2)
    keys_all = 2.5 * jnp.clip(jax.random.normal(first, (SEQ, KV_HEADS, DH), jnp.float32), -6.0, 6.0)
    queries_all = jnp.clip(jax.random.normal(second, (QROWS, HEADS, DH), jnp.float32), -6.0, 6.0)
    return (queries_all, keys_all)


def draw_queries(key, part):
    return draw_together(key)[0].astype(jnp.bfloat16)


def draw_keys(key, part):
    return draw_together(key)[1].astype(jnp.bfloat16)


def levels(stream_key, shape, shards, least, top_value):
    level, own = 1.0, jax.random.fold_in(stream_key, 6)
    for dim, shards_of in shards:
        heights = jnp.exp(jax.random.uniform(jax.random.fold_in(own, dim), (shards_of,), jnp.float32, least / len(shards), top_value / len(shards)))
        level = level * jnp.repeat(heights, shape[dim] // shards_of).reshape([-1 if axis == dim else 1 for axis in range(len(shape))])
    return level


def profile(count, total, limit, lean):
    portions = [(1 << 20) // math.isqrt(grade ** lean) + 1 for grade in range(2, count + 1)]
    spare, counts = total - limit - (count - 1), [1] * (count - 1)
    while spare > 0:
        movable = [i for i in range(count - 1) if counts[i] < limit]
        pool, remaining = sum([portions[i] for i in movable]), spare
        for i in movable:
            addition = min(limit - counts[i], max(1, remaining * portions[i] // pool), spare)
            counts[i] = counts[i] + addition
            spare = spare - addition
    return np.array([limit] + counts)


def ragged(own_key, count, total, limit, lean):
    if count == 2:
        one = jax.random.randint(own_key, (), max(1, total - limit), min(limit, total - 1) + 1)
        return jnp.stack([one, total - one])
    sizes = jnp.asarray(profile(count, total, limit, lean), jnp.int32)
    couples = (count - 1) // 2
    source_of, taker = sizes[1:1 + 2 * couples:2], sizes[2:2 + 2 * couples:2]
    slack = jnp.minimum(source_of - 1, limit - taker)
    shifted = jax.random.randint(jax.random.fold_in(own_key, 1), (couples,), 0, 1 << 20) % (slack + 1)
    sizes = sizes.at[1:1 + 2 * couples:2].set(source_of - shifted).at[2:2 + 2 * couples:2].set(taker + shifted)
    return sizes[jax.random.permutation(jax.random.fold_in(own_key, 2), count)]


def gaussian(key, extent, spread, bound, shards=(), kind=jnp.bfloat16):
    entries = jax.random.normal(key, extent, jnp.float32) * spread
    if len(shards) > 0:
        entries = levels(key, extent, shards, -0.22, 0.18) * entries
    return jnp.clip(entries, min=-bound, max=bound).astype(kind)


def setup_inputs(seed: int = 0) -> dict:
    seeds = jax.random.split(jax.random.key(seed), 5)
    queries = draw_queries(jax.random.fold_in(seeds[4], 71), 0)
    keys = draw_keys(jax.random.fold_in(seeds[4], 71), 0)
    values = gaussian(seeds[2], (SEQ, KV_HEADS, DH), 1.0, 6.0, ((0, 64), (1, 4)))
    doc_lengths = ragged(seeds[3], DOCS, NBLK, MOST_BLK, 2).astype(jnp.int32)
    return {"queries": queries, "keys": keys, "values": values, "doc_lengths": doc_lengths}


NEGATIVE = -1.0e30


def document_of(positions, doc_lengths):
    boundary = (BLOCK * jnp.cumsum(doc_lengths)).astype(jnp.int32)
    return jnp.sum((boundary[None, :] <= positions[:, None]).astype(jnp.int32), axis=1)


def absorb(running, partial_value):
    row_peak = jnp.maximum(running[0], partial_value[0])
    old_factor = jnp.exp(running[0] - row_peak)
    new_factor = jnp.exp(partial_value[0] - row_peak)
    row_total = running[1] * old_factor + partial_value[1] * new_factor
    output = running[2] * old_factor[..., None] + partial_value[2] * new_factor[..., None]
    return (row_peak, row_total, output)


def reference(queries, keys, values, doc_lengths):
    sharing = HEADS // KV_HEADS
    score_scale = DH ** -0.5
    grouped = queries.reshape(QROWS, KV_HEADS, sharing, DH).astype(jnp.float32)
    inner_ids = jnp.arange(CYCLE, dtype=jnp.int32)[:, None, None]
    outer_ids = jnp.arange(OUTER_GROUPS, dtype=jnp.int32)[None, :, None]
    tail_ids = jnp.arange(QT, dtype=jnp.int32)[None, None, :]
    query_pos = ((outer_ids * CYCLE + inner_ids) * KV_DEV + KV_DEV - QT + tail_ids).reshape(-1).astype(jnp.int32)
    query_doc = document_of(query_pos, doc_lengths)
    key_grid = keys.reshape(OUTER_GROUPS * CYCLE, KV_DEV, KV_HEADS, DH)
    value_grid = values.reshape(OUTER_GROUPS * CYCLE, KV_DEV, KV_HEADS, DH)
    segment_ids = jnp.arange(OUTER_GROUPS * CYCLE, dtype=jnp.int32)

    def visit(running, inputs):
        key_tile, value_tile, segment = inputs
        key_pos = (segment * KV_DEV + jnp.arange(KV_DEV, dtype=jnp.int32)).astype(jnp.int32)
        key_doc = document_of(key_pos, doc_lengths)
        alive_mask = (key_pos[None, :] <= query_pos[:, None]) & (key_doc[None, :] == query_doc[:, None])
        scores = jnp.einsum("rhgd,shd->rhgs", grouped, key_tile.astype(jnp.float32), precision=lax.Precision.HIGHEST) * score_scale
        scores = jnp.where(alive_mask[:, None, None, :], scores, NEGATIVE)
        row_peak = jnp.max(scores, axis=3)
        weights = jnp.where(alive_mask[:, None, None, :], jnp.exp(scores - row_peak[..., None]), 0.0)
        row_total = jnp.sum(weights, axis=3)
        rounded = lax.optimization_barrier(weights.astype(jnp.bfloat16))
        output = jnp.einsum("rhgs,shd->rhgd", rounded.astype(jnp.float32), value_tile.astype(jnp.float32), precision=lax.Precision.HIGHEST)
        return absorb(running, (row_peak, row_total, output)), None

    start = (jnp.full((QROWS, KV_HEADS, sharing), NEGATIVE, jnp.float32), jnp.zeros((QROWS, KV_HEADS, sharing), jnp.float32), jnp.zeros((QROWS, KV_HEADS, sharing, DH), jnp.float32))
    running, unused = lax.scan(visit, start, (key_grid, value_grid, segment_ids))
    attended = (running[2] / running[1][..., None]).astype(jnp.bfloat16)
    return attended.reshape(QROWS, HEADS, DH)
```

```python
import functools
import math

import jax
import jax.numpy as jnp
from jax import lax
from jax.experimental import pallas as pl
from jax.experimental.pallas import tpu as pltpu
from jax.sharding import Mesh, PartitionSpec as P

BLOCK = 128
NEGATIVE = -1e30
TAIL = 8
EXTRA = 8


def shifted(part, axis, by):
    size = lax.axis_size(axis)
    return lax.ppermute(part, axis, [(i, (i + by) % size) for i in range(size)])


def attend_kernel(own, factor, chunk, live_ref, q_ref, k_ref, v_ref, out_ref, s_ref):
    kv_count, key_rows, dim = k_ref.shape
    blocks, tail, heads, _ = q_ref.shape
    sharing = heads // kv_count
    wide = tail * sharing
    width = blocks * wide
    n_live = live_ref[0]
    first = live_ref[1]
    chunks = key_rows // chunk
    per = chunk // BLOCK

    @pl.when(own >= n_live)
    def _():
        out_ref[:, :dim, :] = jnp.zeros((blocks, dim, kv_count * wide), jnp.float32)
        row = lax.broadcasted_iota(jnp.int32, (blocks, EXTRA, kv_count * wide), 1)
        out_ref[:, dim:, :] = jnp.where(row == 0, NEGATIVE, 0.0)

    @pl.when(own < n_live)
    def _():
        q_all = q_ref[...].astype(jnp.float32)
        rows = [
            q_all[:, :, h * sharing : (h + 1) * sharing, :]
            .reshape(width, dim)
            .astype(jnp.bfloat16)
            for h in range(kv_count)
        ]

        def score(i, peaks):
            base = pl.multiple_of(i * chunk, chunk)
            new = []
            for h in range(kv_count):
                s = lax.dot_general(
                    k_ref[h, pl.ds(base, chunk), :],
                    rows[h],
                    (((1,), (1,)), ((), ())),
                    preferred_element_type=jnp.float32,
                )
                s_ref[h, pl.ds(base, chunk), :] = s
                peak = peaks[h]
                for b in range(per):
                    top = jnp.max(
                        s[b * BLOCK : (b + 1) * BLOCK].reshape(BLOCK // 8, 8, width), axis=0
                    )
                    peak = jnp.maximum(
                        peak, jnp.where(i * per + b >= first, top, NEGATIVE)
                    )
                new.append(peak)
            return tuple(new)

        none = jnp.full((8, width), NEGATIVE, jnp.float32)
        if own == 0:
            peaks = lax.fori_loop(0, chunks - 1, score, (none,) * kv_count)
            base = (chunks - 1) * chunk
            lane = lax.broadcasted_iota(jnp.int32, (8, width), 1)
            late = lax.broadcasted_iota(jnp.int32, (8, width), 0)
            ahead = (lane < wide) & (late > lane // sharing)
            fixed = []
            for h in range(kv_count):
                s = lax.dot_general(
                    k_ref[h, base:, :],
                    rows[h],
                    (((1,), (1,)), ((), ())),
                    preferred_element_type=jnp.float32,
                )
                corner = jnp.where(ahead, NEGATIVE, s[chunk - 8 :])
                s_ref[h, base : base + chunk - 8, :] = s[: chunk - 8]
                s_ref[h, base + chunk - 8 :, :] = corner
                peak = jnp.maximum(peaks[h], corner)
                for b in range(per):
                    hi = BLOCK if b < per - 1 else BLOCK - 8
                    top = jnp.max(
                        s[b * BLOCK : b * BLOCK + hi].reshape(hi // 8, 8, width), axis=0
                    )
                    peak = jnp.maximum(
                        peak,
                        jnp.where((chunks - 1) * per + b >= first, top, NEGATIVE),
                    )
                fixed.append(peak)
            peaks = tuple(fixed)
        else:
            peaks = lax.fori_loop(0, chunks, score, (none,) * kv_count)
        tops = [jnp.max(p, axis=0, keepdims=True) for p in peaks]

        def gather(i, carry):
            base = pl.multiple_of(i * chunk, chunk)
            new = []
            for h in range(kv_count):
                total, acc = carry[h]
                parts = []
                for b in range(per):
                    s = s_ref[h, pl.ds(base + b * BLOCK, BLOCK), :]
                    ref_row = jnp.where(i * per + b >= first, tops[h], -NEGATIVE)
                    w = jnp.exp2((s - ref_row) * factor)
                    total = total + jnp.sum(w.reshape(BLOCK // 8, 8, width), axis=0)
                    parts.append(w.astype(jnp.bfloat16))
                w = jnp.concatenate(parts, axis=0) if per > 1 else parts[0]
                acc = acc + lax.dot_general(
                    v_ref[h, :, pl.ds(base, chunk)],
                    w,
                    (((1,), (0,)), ((), ())),
                    preferred_element_type=jnp.float32,
                )
                new.append((total, acc))
            return tuple(new)

        zero = (jnp.zeros((8, width), jnp.float32), jnp.zeros((dim, width), jnp.float32))
        sums = lax.fori_loop(0, chunks, gather, (zero,) * kv_count)
        row = lax.broadcasted_iota(jnp.int32, (EXTRA, kv_count * wide), 0)
        for j in range(blocks):
            lanes = slice(j * wide, (j + 1) * wide)
            keep = own + blocks * j < n_live
            o = jnp.concatenate([sums[h][1][:, lanes] for h in range(kv_count)], axis=1)
            m = jnp.concatenate([tops[h][:, lanes] for h in range(kv_count)], axis=1)
            l = jnp.concatenate(
                [jnp.sum(sums[h][0][:, lanes], axis=0, keepdims=True) for h in range(kv_count)],
                axis=1,
            )
            out_ref[j, :dim, :] = jnp.where(keep, o, 0.0)
            out_ref[j, dim:, :] = jnp.where(
                row == 0,
                jnp.where(keep, m, NEGATIVE),
                jnp.where((row == 1) & keep, l, 0.0),
            )


def merge(parts, factor, dim):
    top = functools.reduce(jnp.maximum, [m for _, m, _ in parts])
    o = l = None
    for po, pm, pl_ in parts:
        f = jnp.exp2((pm - top) * factor)
        o = po * f if o is None else o + po * f
        l = pl_ * f if l is None else l + pl_ * f
    return o, top, l


def take(ref, j, dim, valid=None):
    o = ref[j, :dim, :]
    m = ref[j, dim : dim + 1, :]
    l = ref[j, dim + 1 : dim + 2, :]
    if valid is not None:
        o = jnp.where(valid, o, 0.0)
        m = jnp.where(valid, m, NEGATIVE)
        l = jnp.where(valid, l, 0.0)
    return o, m, l


def put(ref, j, dim, o, m, l):
    lanes = m.shape[1]
    row = lax.broadcasted_iota(jnp.int32, (EXTRA, lanes), 0)
    ref[j, :dim, :] = o
    ref[j, dim:, :] = jnp.where(row == 0, m, jnp.where(row == 1, l, 0.0))


def column_kernel(factor, x_ref, *refs):
    parts, out_ref = refs[:-1], refs[-1]
    count, dim = parts[0].shape[0], parts[0].shape[1] - EXTRA
    x = x_ref[0]
    for d in range(count + 1):
        found = []
        for u, ref in enumerate(parts):
            if u == 0:
                if d < count:
                    found.append(take(ref, d, dim))
                continue
            j = d - (x < u).astype(jnp.int32)
            valid = (j >= 0) & (j < count)
            found.append(take(ref, jnp.clip(j, 0, count - 1), dim, valid))
        put(out_ref, d, dim, *merge(found, factor, dim))


def row_kernel(factor, place_ref, *refs):
    parts, out_ref = refs[:-1], refs[-1]
    dim = out_ref.shape[1] - EXTRA
    z, o = place_ref[0], place_ref[1]
    for group in range(out_ref.shape[0]):
        found = []
        for d, ref in enumerate(parts):
            mine = jnp.where(d > z, o + 1, o) == group
            found.append(take(ref, 0, dim, mine))
        put(out_ref, group, dim, *merge(found, factor, dim))


def finish_kernel(factor, kv_count, sharing, a_ref, b_ref, out_ref):
    groups = a_ref.shape[0]
    dim = a_ref.shape[1] - EXTRA
    tail = out_ref.shape[0] // groups
    for g in range(groups):
        o, _, l = merge([take(a_ref, g, dim), take(b_ref, g, dim)], factor, dim)
        res = jnp.transpose(o / l)
        res = res.reshape(kv_count, tail, sharing, dim)
        res = jnp.concatenate([res[h] for h in range(kv_count)], axis=1)
        out_ref[g * tail : (g + 1) * tail] = res.astype(out_ref.dtype)


def vmem(count):
    return [pl.BlockSpec(memory_space=pltpu.VMEM)] * count


def smem():
    return [pl.BlockSpec(memory_space=pltpu.SMEM)]


def body(queries, keys, values, doc_lengths):
    rows, columns = lax.axis_size("z"), lax.axis_size("x")
    o, z, x = lax.axis_index("outer"), lax.axis_index("z"), lax.axis_index("x")
    key_rows, kv_count, dim = keys.shape
    query_rows, heads, _ = queries.shape
    sharing = heads // kv_count
    groups = lax.axis_size("outer")
    lanes = kv_count * TAIL * sharing
    reach = 4
    factor = math.log2(math.e) / math.sqrt(dim)

    segment = (o * rows + z) * columns + x
    ends = jnp.cumsum(doc_lengths)
    blocks = key_rows // BLOCK
    last = segment * blocks + blocks - 1
    start = jnp.max(jnp.where(ends <= last, ends, 0))
    end = jnp.min(jnp.where(ends > last, ends, rows * columns * groups * blocks))
    live = jnp.stack([end // blocks - segment, jnp.maximum(start - segment * blocks, 0)])
    live = live.astype(jnp.int32)

    k_heads = jnp.transpose(keys, (1, 0, 2))
    v_heads = jnp.transpose(values, (1, 2, 0))
    tails = queries.reshape(groups, TAIL, heads, dim)

    held = [lax.dynamic_index_in_dim(tails, o, 0)]
    for d in range(1, reach + 1):
        group = jnp.where(z < d, jnp.minimum(o + 1, groups - 1), o)
        held.append(shifted(lax.dynamic_index_in_dim(tails, group, 0), "z", -d))
    stack = jnp.concatenate(held, axis=0)
    asked = [stack[:reach]]
    for u in range(1, columns):
        asked.append(
            shifted(lax.dynamic_slice_in_dim(stack, (x < u).astype(jnp.int32), reach, 0), "x", -u)
        )

    part = jax.ShapeDtypeStruct((reach, dim + EXTRA, lanes), jnp.float32)
    chunk = 256
    partial = []
    for u in range(columns):
        width = reach * TAIL * sharing
        partial.append(
            pl.pallas_call(
                functools.partial(attend_kernel, u, factor, chunk),
                out_shape=part,
                in_specs=smem() + vmem(3),
                out_specs=vmem(1)[0],
                scratch_shapes=[pltpu.VMEM((kv_count, key_rows, width), jnp.float32)],
                cost_estimate=pl.CostEstimate(
                    flops=4 * kv_count * key_rows * width * dim,
                    bytes_accessed=4 * kv_count * key_rows * dim,
                    transcendentals=kv_count * key_rows * width,
                ),
                compiler_params=pltpu.CompilerParams(vmem_limit_bytes=24 << 20),
                name=f"attend_{u}",
            )(live, asked[u], k_heads, v_heads)
        )
    arrived = [partial[0]] + [shifted(partial[u], "x", u) for u in range(1, columns)]
    column = pl.pallas_call(
        functools.partial(column_kernel, factor),
        out_shape=jax.ShapeDtypeStruct((reach + 1, dim + EXTRA, lanes), jnp.float32),
        in_specs=smem() + vmem(columns),
        out_specs=vmem(1)[0],
        name="merge_columns",
    )(x.reshape(1).astype(jnp.int32), *arrived)
    arrived = [column[:1]] + [shifted(column[d : d + 1], "z", d) for d in range(1, reach + 1)]
    mine = pl.pallas_call(
        functools.partial(row_kernel, factor),
        out_shape=jax.ShapeDtypeStruct((groups, dim + EXTRA, lanes), jnp.float32),
        in_specs=smem() + vmem(reach + 1),
        out_specs=vmem(1)[0],
        name="merge_rows",
    )(jnp.stack([z, o]).astype(jnp.int32), *arrived)
    other = shifted(mine, "outer", 1)
    return pl.pallas_call(
        functools.partial(finish_kernel, factor, kv_count, sharing),
        out_shape=jax.ShapeDtypeStruct(queries.shape, queries.dtype),
        in_specs=vmem(2),
        out_specs=vmem(1)[0],
        name="finish",
    )(mine, other)


def solution(mesh):
    outer, inner, head = (mesh.shape[a] for a in ("outer", "inner", "head"))
    columns = 4
    grid = Mesh(
        mesh.devices.reshape(outer, inner // columns, columns, head),
        ("outer", "z", "x", "head"),
    )
    tails = P(("z", "x"), "head", None)
    rows = P(("outer", "z", "x"), "head", None)
    return jax.shard_map(
        body, mesh=grid, in_specs=(tails, rows, rows, P()), out_specs=tails, check_vma=False
    )
```

```python
import functools
import math

import jax
import jax.numpy as jnp
from jax import lax
from jax.experimental import pallas as pl
from jax.experimental.pallas import tpu as pltpu
from jax.sharding import Mesh, PartitionSpec as P

BLOCK = 128
NEGATIVE = -1e30
TAIL = 8
EXTRA = 8
COLUMNS = 4
REACH = 4


def shifted(part, axes, by):
    size = lax.axis_size(axes)
    return lax.ppermute(part, axes, [(i, (i + by) % size) for i in range(size)])


def own_kernel(kv_count, o_ref, q_ref, out_ref):
    tail = TAIL
    sharing = q_ref.shape[1] // kv_count
    mine = q_ref[pl.ds(o_ref[0] * tail, tail)].astype(jnp.float32)
    rows = [
        mine[:, h * sharing : (h + 1) * sharing, :].reshape(tail * sharing, -1)
        for h in range(kv_count)
    ]
    out_ref[...] = jnp.transpose(jnp.concatenate(rows, axis=0)).astype(out_ref.dtype)


def stack_kernel(*refs):
    blocks, out_ref = refs[:-1], refs[-1]
    kv_count = out_ref.shape[0]
    wide = out_ref.shape[2] // len(blocks)
    for h in range(kv_count):
        out_ref[h] = jnp.concatenate(
            [b[:, h * wide : (h + 1) * wide] for b in blocks], axis=1
        )


def attend_kernel(own, factor, live_ref, q_ref, k_ref, v_ref, out_ref, s_ref):
    kv_count, key_rows, dim = k_ref.shape
    width = q_ref.shape[2]
    blocks = out_ref.shape[0]
    wide = width // blocks
    sharing = wide // TAIL
    n_live = live_ref[0]
    first = live_ref[1]
    count = key_rows // BLOCK

    @pl.when(own >= n_live)
    def _():
        out_ref[:, :dim, :] = jnp.zeros((blocks, dim, kv_count * wide), jnp.float32)
        row = lax.broadcasted_iota(jnp.int32, (blocks, EXTRA, kv_count * wide), 1)
        out_ref[:, dim:, :] = jnp.where(row == 0, NEGATIVE, 0.0)

    @pl.when(own < n_live)
    def _():
        tops, totals, outputs = [], [], []
        for h in range(kv_count):
            s = jnp.dot(k_ref[h], q_ref[h], preferred_element_type=jnp.float32)
            s_ref[h] = s
            peak = jnp.full((8, width), NEGATIVE, jnp.float32)
            for b in range(count):
                rows = s[b * BLOCK : (b + 1) * BLOCK]
                if own == 0 and b == count - 1:
                    lane = lax.broadcasted_iota(jnp.int32, (8, width), 1)
                    late = lax.broadcasted_iota(jnp.int32, (8, width), 0)
                    ahead = (lane < wide) & (late > lane // sharing)
                    corner = jnp.where(ahead, NEGATIVE, rows[BLOCK - 8 :])
                    s_ref[h, key_rows - 8 :, :] = corner
                    peak = jnp.maximum(peak, corner)
                    rows = rows[: BLOCK - 8]
                top = jnp.max(rows.reshape(-1, 8, width), axis=0)
                peak = jnp.maximum(peak, jnp.where(b >= first, top, NEGATIVE))
            tops.append(jnp.max(peak, axis=0, keepdims=True))
        for h in range(kv_count):
            total = jnp.zeros((8, width), jnp.float32)
            parts = []
            for b in range(count):
                s = s_ref[h, b * BLOCK : (b + 1) * BLOCK, :]
                level = jnp.where(b >= first, tops[h], -NEGATIVE)
                w = jnp.exp2((s - level) * factor)
                total = total + jnp.sum(w.reshape(-1, 8, width), axis=0)
                parts.append(w.astype(jnp.bfloat16))
            totals.append(jnp.sum(total, axis=0, keepdims=True))
            outputs.append(
                jnp.dot(v_ref[h], jnp.concatenate(parts, axis=0), preferred_element_type=jnp.float32)
            )
        row = lax.broadcasted_iota(jnp.int32, (EXTRA, kv_count * wide), 0)
        for j in range(blocks):
            lanes = slice(j * wide, (j + 1) * wide)
            keep = own + blocks * j < n_live
            o = jnp.concatenate([a[:, lanes] for a in outputs], axis=1)
            m = jnp.concatenate([a[:, lanes] for a in tops], axis=1)
            l = jnp.concatenate([a[:, lanes] for a in totals], axis=1)
            out_ref[j, :dim, :] = jnp.where(keep, o, 0.0)
            out_ref[j, dim:, :] = jnp.where(
                row == 0,
                jnp.where(keep, m, NEGATIVE),
                jnp.where((row == 1) & keep, l, 0.0),
            )


def merge(parts, factor):
    top = functools.reduce(jnp.maximum, [m for _, m, _ in parts])
    o = l = None
    for po, pm, pt in parts:
        f = jnp.exp2((pm - top) * factor)
        o = po * f if o is None else o + po * f
        l = pt * f if l is None else l + pt * f
    return o, top, l


def column_kernel(factor, *refs):
    parts, outs = refs[:COLUMNS], refs[COLUMNS:]
    dim = outs[0].shape[0] - EXTRA
    for j, out in enumerate(outs):
        found = [(p[j, :dim], p[j, dim : dim + 1], p[j, dim + 1 : dim + 2]) for p in parts]
        o, m, l = merge(found, factor)
        row = lax.broadcasted_iota(jnp.int32, (EXTRA, m.shape[1]), 0)
        out[:dim] = o
        out[dim:] = jnp.where(row == 0, m, jnp.where(row == 1, l, 0.0))


def finish_kernel(factor, kv_count, *refs):
    parts, out_ref = refs[:-1], refs[-1]
    dim = out_ref.shape[2]
    found = [(p[:dim], p[dim : dim + 1], p[dim + 1 : dim + 2]) for p in parts]
    o, _, l = merge(found, factor)
    res = jnp.transpose(o / l).reshape(kv_count, TAIL, -1, dim)
    out_ref[...] = jnp.concatenate([res[h] for h in range(kv_count)], axis=1).astype(out_ref.dtype)


def on_chip(count):
    return [pl.BlockSpec(memory_space=pltpu.VMEM)] * count


def room(mebibytes):
    return pltpu.CompilerParams(vmem_limit_bytes=mebibytes << 20)


def scalars():
    return [pl.BlockSpec(memory_space=pltpu.SMEM)]


def body(queries, keys, values, doc_lengths):
    rows, columns, groups = lax.axis_size("z"), lax.axis_size("x"), lax.axis_size("outer")
    o, z, x = lax.axis_index("outer"), lax.axis_index("z"), lax.axis_index("x")
    key_rows, kv_count, dim = keys.shape
    heads = queries.shape[1]
    sharing = heads // kv_count
    lanes = kv_count * TAIL * sharing
    width = REACH * TAIL * sharing
    factor = math.log2(math.e) / math.sqrt(dim)

    own = pl.pallas_call(
        functools.partial(own_kernel, kv_count),
        out_shape=jax.ShapeDtypeStruct((dim, lanes), queries.dtype),
        in_specs=scalars() + on_chip(1),
        out_specs=on_chip(1)[0],
        compiler_params=room(4),
        name="own_tails",
    )(o.reshape(1).astype(jnp.int32), queries)
    held = [own] + [shifted(own, ("outer", "z"), -j) for j in range(1, REACH)]

    segment = (o * rows + z) * columns + x
    blocks = key_rows // BLOCK
    ends = jnp.cumsum(doc_lengths)
    last = segment * blocks + blocks - 1
    start = jnp.max(jnp.where(ends <= last, ends, 0))
    end = jnp.min(jnp.where(ends > last, ends, rows * columns * groups * blocks))
    live = jnp.stack([end // blocks - segment, jnp.maximum(start - segment * blocks, 0)])
    live = live.astype(jnp.int32)
    k_heads = jnp.transpose(keys, (1, 0, 2))
    v_heads = jnp.transpose(values, (1, 2, 0))
    held, live, k_heads, v_heads = lax.optimization_barrier((held, live, k_heads, v_heads))

    stack = pl.pallas_call(
        stack_kernel,
        out_shape=jax.ShapeDtypeStruct((kv_count, dim, width), queries.dtype),
        in_specs=on_chip(REACH),
        out_specs=on_chip(1)[0],
        compiler_params=room(4),
        name="stack_tails",
    )(*held)
    everywhere = ("outer", "z", "x")
    asked = [stack] + [shifted(stack, everywhere, -u) for u in range(1, columns)]

    partial = []
    for u in range(columns):
        block = asked[u]
        if u == 1:
            block, _ = lax.optimization_barrier((block, partial[0]))
        partial.append(
            pl.pallas_call(
                functools.partial(attend_kernel, u, factor),
                out_shape=jax.ShapeDtypeStruct((REACH, dim + EXTRA, lanes), jnp.float32),
                in_specs=scalars() + on_chip(3),
                out_specs=on_chip(1)[0],
                scratch_shapes=[pltpu.VMEM((kv_count, key_rows, width), jnp.float32)],
                cost_estimate=pl.CostEstimate(
                    flops=4 * kv_count * key_rows * width * dim,
                    bytes_accessed=4 * kv_count * key_rows * dim,
                    transcendentals=kv_count * key_rows * width,
                ),
                compiler_params=room(16),
                name=f"attend_{u}",
            )(live, block, k_heads, v_heads)
        )
    arrived = [partial[0]] + [shifted(partial[u], everywhere, u) for u in range(1, columns)]
    column = pl.pallas_call(
        functools.partial(column_kernel, factor),
        out_shape=[jax.ShapeDtypeStruct((dim + EXTRA, lanes), jnp.float32)] * REACH,
        in_specs=on_chip(columns),
        out_specs=on_chip(REACH),
        compiler_params=room(4),
        name="merge_columns",
    )(*arrived)
    arrived = [column[0]] + [shifted(column[j], ("outer", "z"), j) for j in range(1, REACH)]
    mine = pl.pallas_call(
        functools.partial(finish_kernel, factor, kv_count),
        out_shape=jax.ShapeDtypeStruct((TAIL, heads, dim), queries.dtype),
        in_specs=on_chip(REACH),
        out_specs=on_chip(1)[0],
        compiler_params=room(4),
        name="finish",
    )(*arrived)
    other = shifted(mine, "outer", 1)
    first = jnp.where(o == 0, mine, other)
    second = jnp.where(o == 0, other, mine)
    return jnp.concatenate([first, second], axis=0)


def solution(mesh):
    outer, inner, head = (mesh.shape[a] for a in ("outer", "inner", "head"))
    grid = Mesh(
        mesh.devices.reshape(outer, inner // COLUMNS, COLUMNS, head),
        ("outer", "z", "x", "head"),
    )
    tails = P(("z", "x"), "head", None)
    rows = P(("outer", "z", "x"), "head", None)
    return jax.shard_map(
        body, mesh=grid, in_specs=(tails, rows, rows, P()), out_specs=tails, check_vma=False
    )
```

```python
import functools
import math

import jax
import jax.numpy as jnp
from jax import lax
from jax.experimental import pallas as pl
from jax.experimental.pallas import tpu as pltpu
from jax.sharding import Mesh, PartitionSpec as P

BLOCK = 128
NEGATIVE = -1e30
TAIL = 8
NOTHING = -32768.0
EXTRA = 8
CODED = 16
COLUMNS = 4
REACH = 4


def shifted(part, axes, by):
    size = lax.axis_size(axes)
    return lax.ppermute(part, axes, [(i, (i + by) % size) for i in range(size)])


def own_kernel(kv_count, o_ref, q_ref, out_ref):
    tail = TAIL
    sharing = q_ref.shape[1] // kv_count
    mine = q_ref[pl.ds(o_ref[0] * tail, tail)].astype(jnp.float32)
    rows = [
        mine[:, h * sharing : (h + 1) * sharing, :].reshape(tail * sharing, -1)
        for h in range(kv_count)
    ]
    out_ref[...] = jnp.transpose(jnp.concatenate(rows, axis=0)).astype(out_ref.dtype)


def stack_kernel(*refs):
    blocks, out_ref = refs[:-1], refs[-1]
    kv_count = out_ref.shape[0]
    wide = out_ref.shape[2] // len(blocks)
    for h in range(kv_count):
        out_ref[h] = jnp.concatenate(
            [b[:, h * wide : (h + 1) * wide] for b in blocks], axis=1
        )


def place_of(blocks, segment_ref, lengths_ref):
    segment = segment_ref[0]
    last = segment * blocks + (blocks - 1)
    edge, start, end = jnp.int32(0), jnp.int32(0), jnp.int32(1 << 24)
    for k in range(lengths_ref.shape[0]):
        edge = edge + lengths_ref[k]
        start = jnp.where(edge <= last, edge, start)
        end = jnp.where(edge > last, jnp.minimum(end, edge), end)
    return lax.div(end, jnp.int32(blocks)) - segment, start - segment * blocks


def write_exact(ref, o, m, l):
    dim = o.shape[0]
    row = lax.broadcasted_iota(jnp.int32, (EXTRA, o.shape[1]), 0)
    ref[:dim] = o
    ref[dim:] = jnp.where(row == 0, m, jnp.where(row == 1, l, 0.0))


def read_exact(ref, dim):
    return ref[:dim], ref[dim : dim + 1], ref[dim + 1 : dim + 2]


def write_coded(ref, o, m, l):
    dim = o.shape[0]
    most = jnp.maximum(jnp.max(jnp.abs(o), axis=0, keepdims=True), 1e-30)
    power = jnp.floor(jnp.log2(most) + 1e-3) + 1.0
    code = jnp.clip(jnp.floor(o * jnp.exp2(15.0 - power) + 0.5), -32767.0, 32767.0)
    high = jnp.floor(l * 2.0)
    low = jnp.floor((l * 2.0 - high) * 32768.0)
    row = lax.broadcasted_iota(jnp.int32, (CODED, o.shape[1]), 0)
    tail = jnp.where(row == 0, m, jnp.where(row == 1, high, jnp.where(row == 2, low, power)))
    ref[:dim] = code.astype(jnp.int32).astype(jnp.int16)
    ref[dim:] = tail.astype(jnp.int32).astype(jnp.int16)


def read_coded(ref, dim):
    tail = ref[dim:].astype(jnp.int32).astype(jnp.float32)
    m, high, low, power = (tail[k : k + 1] for k in range(4))
    o = ref[:dim].astype(jnp.int32).astype(jnp.float32) * jnp.exp2(power - 15.0)
    return o, m, (high + low * (1.0 / 32768.0)) * 0.5


def attend_kernel(own, factor, segment_ref, lengths_ref, q_ref, k_ref, v_ref, out_ref, s_ref):
    kv_count, key_rows, dim = k_ref.shape
    width = q_ref.shape[2]
    blocks = out_ref.shape[0]
    wide = width // blocks
    sharing = wide // TAIL
    lanes = kv_count * wide
    count = key_rows // BLOCK
    n_live, first = place_of(count, segment_ref, lengths_ref)
    write = write_exact if own == 0 else write_coded

    @pl.when(own >= n_live)
    def _():
        none = jnp.zeros((1, lanes), jnp.float32)
        for j in range(blocks):
            write(out_ref.at[j], jnp.zeros((dim, lanes), jnp.float32), none + NOTHING, none)

    @pl.when(own < n_live)
    def _():
        tops, totals, outputs = [], [], []
        for h in range(kv_count):
            s = jnp.dot(k_ref[h], q_ref[h], preferred_element_type=jnp.float32)
            s_ref[h] = s
            peak = jnp.full((8, width), NEGATIVE, jnp.float32)
            for b in range(count):
                rows = s[b * BLOCK : (b + 1) * BLOCK]
                if own == 0 and b == count - 1:
                    lane = lax.broadcasted_iota(jnp.int32, (8, width), 1)
                    late = lax.broadcasted_iota(jnp.int32, (8, width), 0)
                    ahead = (lane < wide) & (late > lane // sharing)
                    corner = jnp.where(ahead, NEGATIVE, rows[BLOCK - 8 :])
                    s_ref[h, key_rows - 8 :, :] = corner
                    peak = jnp.maximum(peak, corner)
                    rows = rows[: BLOCK - 8]
                top = jnp.max(rows.reshape(-1, 8, width), axis=0)
                peak = jnp.maximum(peak, jnp.where(b >= first, top, NEGATIVE))
            tops.append(jnp.max(peak, axis=0, keepdims=True))
        for h in range(kv_count):
            total = jnp.zeros((8, width), jnp.float32)
            parts = []
            for b in range(count):
                s = s_ref[h, b * BLOCK : (b + 1) * BLOCK, :]
                level = jnp.where(b >= first, tops[h], -NEGATIVE)
                w = jnp.exp2((s - level) * factor)
                total = total + jnp.sum(w.reshape(-1, 8, width), axis=0)
                parts.append(w.astype(jnp.bfloat16))
            totals.append(jnp.sum(total, axis=0, keepdims=True))
            outputs.append(
                jnp.dot(v_ref[h], jnp.concatenate(parts, axis=0), preferred_element_type=jnp.float32)
            )
        for j in range(blocks):
            here = slice(j * wide, (j + 1) * wide)
            keep = own + blocks * j < n_live
            o = jnp.concatenate([a[:, here] for a in outputs], axis=1)
            m = jnp.concatenate([a[:, here] for a in tops], axis=1) * factor
            l = jnp.concatenate([a[:, here] for a in totals], axis=1)
            whole = jnp.ceil(m)
            f = jnp.where(keep, jnp.exp2(m - whole), 0.0)
            write(
                out_ref.at[j], jnp.where(keep, o * f, 0.0), jnp.where(keep, whole, NOTHING), l * f
            )


def merge(parts):
    top = functools.reduce(jnp.maximum, [m for _, m, _ in parts])
    o = l = None
    for po, pm, pt in parts:
        f = jnp.exp2(pm - top)
        o = po * f if o is None else o + po * f
        l = pt * f if l is None else l + pt * f
    return o, top, l


def column_kernel(*refs):
    parts, outs = refs[:COLUMNS], refs[COLUMNS:]
    dim = outs[0].shape[0] - EXTRA
    for j, out in enumerate(outs):
        found = [read_exact(parts[0].at[j], dim)] + [read_coded(p.at[j], dim) for p in parts[1:]]
        write = write_exact if j == 0 else write_coded
        write(out, *merge(found))


def finish_kernel(kv_count, *refs):
    parts, out_ref = refs[:-1], refs[-1]
    dim = out_ref.shape[2]
    found = [read_exact(parts[0], dim)] + [read_coded(p, dim) for p in parts[1:]]
    o, _, l = merge(found)
    res = jnp.transpose(o / l).reshape(kv_count, TAIL, -1, dim)
    out_ref[...] = jnp.concatenate([res[h] for h in range(kv_count)], axis=1).astype(out_ref.dtype)


def on_chip(count):
    return [pl.BlockSpec(memory_space=pltpu.VMEM)] * count


def room(mebibytes):
    return pltpu.CompilerParams(vmem_limit_bytes=mebibytes << 20)


def scalars():
    return [pl.BlockSpec(memory_space=pltpu.SMEM)]


def body(queries, keys, values, doc_lengths):
    rows, columns = lax.axis_size("z"), lax.axis_size("x")
    o, z, x = lax.axis_index("outer"), lax.axis_index("z"), lax.axis_index("x")
    key_rows, kv_count, dim = keys.shape
    heads = queries.shape[1]
    sharing = heads // kv_count
    lanes = kv_count * TAIL * sharing
    width = REACH * TAIL * sharing
    factor = math.log2(math.e) / math.sqrt(dim)

    own = pl.pallas_call(
        functools.partial(own_kernel, kv_count),
        out_shape=jax.ShapeDtypeStruct((dim, lanes), queries.dtype),
        in_specs=scalars() + on_chip(1),
        out_specs=on_chip(1)[0],
        compiler_params=room(4),
        name="own_tails",
    )(o.reshape(1).astype(jnp.int32), queries)
    held = [own] + [shifted(own, ("outer", "z"), -j) for j in range(1, REACH)]

    segment = ((o * rows + z) * columns + x).reshape(1).astype(jnp.int32)
    k_heads = jnp.transpose(keys, (1, 0, 2))
    held, k_heads, values = lax.optimization_barrier((held, k_heads, values))
    v_heads = jnp.transpose(values, (1, 2, 0))

    stack = pl.pallas_call(
        stack_kernel,
        out_shape=jax.ShapeDtypeStruct((kv_count, dim, width), queries.dtype),
        in_specs=on_chip(REACH),
        out_specs=on_chip(1)[0],
        compiler_params=room(4),
        name="stack_tails",
    )(*held)
    everywhere = ("outer", "z", "x")
    asked = [stack] + [shifted(stack, everywhere, -u) for u in range(1, columns)]

    exact = jax.ShapeDtypeStruct((REACH, dim + EXTRA, lanes), jnp.float32)
    coded = jax.ShapeDtypeStruct((REACH, dim + CODED, lanes), jnp.int16)
    partial = []
    for u in range(columns):
        block = asked[u]
        if u == 1:
            block, _ = lax.optimization_barrier((block, partial[0]))
        partial.append(
            pl.pallas_call(
                functools.partial(attend_kernel, u, factor),
                out_shape=exact if u == 0 else coded,
                in_specs=scalars() * 2 + on_chip(3),
                out_specs=on_chip(1)[0],
                scratch_shapes=[pltpu.VMEM((kv_count, key_rows, width), jnp.float32)],
                cost_estimate=pl.CostEstimate(
                    flops=4 * kv_count * key_rows * width * dim,
                    bytes_accessed=4 * kv_count * key_rows * dim,
                    transcendentals=kv_count * key_rows * width,
                ),
                compiler_params=room(16),
                name=f"attend_{u}",
            )(segment, doc_lengths, block, k_heads, v_heads)
        )
    arrived = [partial[0]] + [shifted(partial[u], everywhere, u) for u in range(1, columns)]
    column = pl.pallas_call(
        column_kernel,
        out_shape=[jax.ShapeDtypeStruct((dim + EXTRA, lanes), jnp.float32)]
        + [jax.ShapeDtypeStruct((dim + CODED, lanes), jnp.int16)] * (REACH - 1),
        in_specs=on_chip(columns),
        out_specs=on_chip(REACH),
        compiler_params=room(4),
        name="merge_columns",
    )(*arrived)
    arrived = [column[0]] + [shifted(column[j], ("outer", "z"), j) for j in range(1, REACH)]
    mine = pl.pallas_call(
        functools.partial(finish_kernel, kv_count),
        out_shape=jax.ShapeDtypeStruct((TAIL, heads, dim), queries.dtype),
        in_specs=on_chip(REACH),
        out_specs=on_chip(1)[0],
        compiler_params=room(4),
        name="finish",
    )(*arrived)
    other = shifted(mine, "outer", 1)
    first = jnp.where(o == 0, mine, other)
    second = jnp.where(o == 0, other, mine)
    return jnp.concatenate([first, second], axis=0)


def solution(mesh):
    outer, inner, head = (mesh.shape[a] for a in ("outer", "inner", "head"))
    grid = Mesh(
        mesh.devices.reshape(outer, inner // COLUMNS, COLUMNS, head),
        ("outer", "z", "x", "head"),
    )
    tails = P(("z", "x"), "head", None)
    rows = P(("outer", "z", "x"), "head", None)
    return jax.shard_map(
        body, mesh=grid, in_specs=(tails, rows, rows, P()), out_specs=tails, check_vma=False
    )
```

```python
import functools
import math

import jax
import jax.numpy as jnp
from jax import lax
from jax.experimental import pallas as pl
from jax.experimental.pallas import tpu as pltpu
from jax.sharding import Mesh, PartitionSpec as P

BLOCK = 128
STEP = 512
NEGATIVE = -1e30
TAIL = 8
NOTHING = -32768.0
EXTRA = 8
CODED = 16
COLUMNS = 4
REACH = 4


def shifted(part, axes, by):
    size = lax.axis_size(axes)
    return lax.ppermute(part, axes, [(i, (i + by) % size) for i in range(size)])


def mask_kernel(blocks, lengths_ref, live_ref):
    rows, columns = lax.axis_size("z"), lax.axis_size("x")
    segment = (lax.axis_index("outer") * rows + lax.axis_index("z")) * columns + lax.axis_index("x")
    count = lengths_ref.shape[1]
    lengths = jnp.broadcast_to(lengths_ref[...].astype(jnp.float32), (count, count))
    upto = lax.broadcasted_iota(jnp.int32, (count, count), 0)
    which = lax.broadcasted_iota(jnp.int32, (count, count), 1)
    edges = jnp.sum(jnp.where(which <= upto, lengths, 0.0), axis=1, keepdims=True)
    here = (segment * blocks).astype(jnp.float32)
    last = here + (blocks - 1.0)
    start = jnp.max(jnp.where(edges <= last, edges, 0.0), axis=0, keepdims=True)
    end = jnp.min(jnp.where(edges > last, edges, 1e9), axis=0, keepdims=True)
    n_live = jnp.floor(end * (1.0 / blocks)) - segment.astype(jnp.float32)
    row = lax.broadcasted_iota(jnp.int32, live_ref.shape, 0)
    live_ref[...] = jnp.where(row == 0, n_live, start - here)


def own_kernel(kv_count, o_ref, q_ref, out_ref):
    tail = TAIL
    sharing = q_ref.shape[1] // kv_count
    mine = q_ref[pl.ds(o_ref[0] * tail, tail)].astype(jnp.float32)
    rows = [
        mine[:, h * sharing : (h + 1) * sharing, :].reshape(tail * sharing, -1)
        for h in range(kv_count)
    ]
    out_ref[...] = jnp.transpose(jnp.concatenate(rows, axis=0)).astype(out_ref.dtype)


def stack_kernel(*refs):
    blocks, out_ref = refs[:-1], refs[-1]
    kv_count = out_ref.shape[0]
    wide = out_ref.shape[2] // len(blocks)
    for h in range(kv_count):
        out_ref[h] = jnp.concatenate(
            [b[:, h * wide : (h + 1) * wide] for b in blocks], axis=1
        )


def write_exact(ref, o, m, l):
    dim = o.shape[0]
    row = lax.broadcasted_iota(jnp.int32, (EXTRA, o.shape[1]), 0)
    ref[:dim] = o
    ref[dim:] = jnp.where(row == 0, m, jnp.where(row == 1, l, 0.0))


def read_exact(ref, dim):
    return ref[:dim], ref[dim : dim + 1], ref[dim + 1 : dim + 2]


def write_coded(ref, o, m, l):
    dim = o.shape[0]
    most = jnp.maximum(jnp.max(jnp.abs(o), axis=0, keepdims=True), 1e-30)
    power = jnp.floor(jnp.log2(most) + 1e-3) + 1.0
    code = jnp.clip(jnp.floor(o * jnp.exp2(15.0 - power) + 0.5), -32767.0, 32767.0)
    high = jnp.floor(l * 2.0)
    low = jnp.floor((l * 2.0 - high) * 32768.0)
    row = lax.broadcasted_iota(jnp.int32, (CODED, o.shape[1]), 0)
    tail = jnp.where(row == 0, m, jnp.where(row == 1, high, jnp.where(row == 2, low, power)))
    ref[:dim] = code.astype(jnp.int32).astype(jnp.int16)
    ref[dim:] = tail.astype(jnp.int32).astype(jnp.int16)


def read_coded(ref, dim):
    tail = ref[dim:].astype(jnp.int32).astype(jnp.float32)
    m, high, low, power = (tail[k : k + 1] for k in range(4))
    o = ref[:dim].astype(jnp.int32).astype(jnp.float32) * jnp.exp2(power - 15.0)
    return o, m, (high + low * (1.0 / 32768.0)) * 0.5


def attend_kernel(own, factor, live_ref, q_ref, k_ref, v_ref, out_ref, s_ref):
    kv_count, key_rows, dim = k_ref.shape
    width = q_ref.shape[2]
    blocks = out_ref.shape[0]
    wide = width // blocks
    sharing = wide // TAIL
    lanes = kv_count * wide
    count = key_rows // BLOCK
    n_live, first = live_ref[0:1, 0:1], live_ref[1:2, 0:1]
    some = jnp.max(live_ref[0:1, :])
    write = write_exact if own == 0 else write_coded

    @pl.when(own >= some)
    def _():
        none = jnp.zeros((1, lanes), jnp.float32)
        for j in range(blocks):
            write(out_ref.at[j], jnp.zeros((dim, lanes), jnp.float32), none + NOTHING, none)

    @pl.when(own < some)
    def _():
        per = STEP // BLOCK
        steps = key_rows // STEP

        def score(h, c):
            s = jnp.dot(
                k_ref[h, c * STEP : (c + 1) * STEP, :], q_ref[h], preferred_element_type=jnp.float32
            )
            s_ref[h, c * STEP : (c + 1) * STEP, :] = s
            peak = jnp.full((8, width), NEGATIVE, jnp.float32)
            for b in range(per):
                rows = s[b * BLOCK : (b + 1) * BLOCK]
                if own == 0 and c * per + b == count - 1:
                    lane = lax.broadcasted_iota(jnp.int32, (8, width), 1)
                    late = lax.broadcasted_iota(jnp.int32, (8, width), 0)
                    ahead = (lane < wide) & (late > lane // sharing)
                    corner = jnp.where(ahead, NEGATIVE, rows[BLOCK - 8 :])
                    s_ref[h, key_rows - 8 :, :] = corner
                    peak = jnp.maximum(peak, corner)
                    rows = rows[: BLOCK - 8]
                top = jnp.max(rows.reshape(-1, 8, width), axis=0)
                peak = jnp.maximum(peak, jnp.where(c * per + b >= first, top, NEGATIVE))
            return peak

        def weigh(h, c, top, total):
            parts = []
            for b in range(c * per, (c + 1) * per):
                s = s_ref[h, b * BLOCK : (b + 1) * BLOCK, :]
                w = jnp.exp2((s - jnp.where(b >= first, top, -NEGATIVE)) * factor)
                total = total + jnp.sum(w.reshape(-1, 8, width), axis=0)
                parts.append(w.astype(jnp.bfloat16))
            return parts, total

        tops, totals, outputs = [], [], []
        peaks = [score(0, c) for c in range(steps)]
        for h in range(kv_count):
            tops.append(jnp.max(functools.reduce(jnp.maximum, peaks), axis=0, keepdims=True))
            peaks, parts, total = [], [], jnp.zeros((8, width), jnp.float32)
            for c in range(steps):
                more, total = weigh(h, c, tops[h], total)
                parts += more
                if h + 1 < kv_count:
                    peaks.append(score(h + 1, c))
            totals.append(jnp.sum(total, axis=0, keepdims=True))
            outputs.append(
                jnp.dot(v_ref[h], jnp.concatenate(parts, axis=0), preferred_element_type=jnp.float32)
            )
        for j in range(blocks):
            here = slice(j * wide, (j + 1) * wide)
            keep = own + blocks * j < n_live
            o = jnp.concatenate([a[:, here] for a in outputs], axis=1)
            m = jnp.concatenate([a[:, here] for a in tops], axis=1) * factor
            l = jnp.concatenate([a[:, here] for a in totals], axis=1)
            whole = jnp.ceil(m)
            f = jnp.where(keep, jnp.exp2(m - whole), 0.0)
            write(
                out_ref.at[j], jnp.where(keep, o * f, 0.0), jnp.where(keep, whole, NOTHING), l * f
            )


def merge(parts):
    top = functools.reduce(jnp.maximum, [m for _, m, _ in parts])
    o = l = None
    for po, pm, pt in parts:
        f = jnp.exp2(pm - top)
        o = po * f if o is None else o + po * f
        l = pt * f if l is None else l + pt * f
    return o, top, l


def column_kernel(*refs):
    parts, outs = refs[:COLUMNS], refs[COLUMNS:]
    dim = outs[0].shape[0] - EXTRA
    for j, out in enumerate(outs):
        found = [read_exact(parts[0].at[j], dim)] + [read_coded(p.at[j], dim) for p in parts[1:]]
        write = write_exact if j == 0 else write_coded
        write(out, *merge(found))


def finish_kernel(kv_count, *refs):
    parts, out_ref = refs[:-1], refs[-1]
    dim = out_ref.shape[2]
    found = [read_exact(parts[0], dim)] + [read_coded(p, dim) for p in parts[1:]]
    o, _, l = merge(found)
    res = jnp.transpose(o / l).reshape(kv_count, TAIL, -1, dim)
    out_ref[...] = jnp.concatenate([res[h] for h in range(kv_count)], axis=1).astype(out_ref.dtype)


def on_chip(count):
    return [pl.BlockSpec(memory_space=pltpu.VMEM)] * count


def room(mebibytes):
    return pltpu.CompilerParams(vmem_limit_bytes=mebibytes << 20)


def scalars():
    return [pl.BlockSpec(memory_space=pltpu.SMEM)]


def body(queries, keys, values, doc_lengths):
    columns = lax.axis_size("x")
    o = lax.axis_index("outer")
    key_rows, kv_count, dim = keys.shape
    heads = queries.shape[1]
    sharing = heads // kv_count
    lanes = kv_count * TAIL * sharing
    width = REACH * TAIL * sharing
    factor = math.log2(math.e) / math.sqrt(dim)

    own = pl.pallas_call(
        functools.partial(own_kernel, kv_count),
        out_shape=jax.ShapeDtypeStruct((dim, lanes), queries.dtype),
        in_specs=scalars() + on_chip(1),
        out_specs=on_chip(1)[0],
        compiler_params=room(4),
        name="own_tails",
    )(o.reshape(1).astype(jnp.int32), queries)
    held = [own] + [shifted(own, ("outer", "z"), -j) for j in range(1, REACH)]

    live = pl.pallas_call(
        functools.partial(mask_kernel, key_rows // BLOCK),
        out_shape=jax.ShapeDtypeStruct((8, 128), jnp.float32),
        in_specs=on_chip(1),
        out_specs=on_chip(1)[0],
        compiler_params=room(4),
        name="mask",
    )(doc_lengths.reshape(1, -1))
    k_heads = jnp.transpose(keys, (1, 0, 2))
    v_heads = jnp.transpose(values, (1, 2, 0))
    held, live, k_heads, v_heads = lax.optimization_barrier((held, live, k_heads, v_heads))

    stack = pl.pallas_call(
        stack_kernel,
        out_shape=jax.ShapeDtypeStruct((kv_count, dim, width), queries.dtype),
        in_specs=on_chip(REACH),
        out_specs=on_chip(1)[0],
        compiler_params=room(4),
        name="stack_tails",
    )(*held)
    everywhere = ("outer", "z", "x")
    asked = [stack] + [shifted(stack, everywhere, -u) for u in range(1, columns)]

    exact = jax.ShapeDtypeStruct((REACH, dim + EXTRA, lanes), jnp.float32)
    coded = jax.ShapeDtypeStruct((REACH, dim + CODED, lanes), jnp.int16)
    partial = []
    for u in range(columns):
        block = asked[u]
        if u == 1:
            block, _ = lax.optimization_barrier((block, partial[0]))
        partial.append(
            pl.pallas_call(
                functools.partial(attend_kernel, u, factor),
                out_shape=exact if u == 0 else coded,
                in_specs=on_chip(4),
                out_specs=on_chip(1)[0],
                scratch_shapes=[pltpu.VMEM((kv_count, key_rows, width), jnp.float32)],
                cost_estimate=pl.CostEstimate(
                    flops=4 * kv_count * key_rows * width * dim,
                    bytes_accessed=4 * kv_count * key_rows * dim,
                    transcendentals=kv_count * key_rows * width,
                ),
                compiler_params=room(16),
                name=f"attend_{u}",
            )(live, block, k_heads, v_heads)
        )
    arrived = [partial[0]] + [shifted(partial[u], everywhere, u) for u in range(1, columns)]
    column = pl.pallas_call(
        column_kernel,
        out_shape=[jax.ShapeDtypeStruct((dim + EXTRA, lanes), jnp.float32)]
        + [jax.ShapeDtypeStruct((dim + CODED, lanes), jnp.int16)] * (REACH - 1),
        in_specs=on_chip(columns),
        out_specs=on_chip(REACH),
        compiler_params=room(4),
        name="merge_columns",
    )(*arrived)
    arrived = [column[0]] + [shifted(column[j], ("outer", "z"), j) for j in range(1, REACH)]
    mine = pl.pallas_call(
        functools.partial(finish_kernel, kv_count),
        out_shape=jax.ShapeDtypeStruct((TAIL, heads, dim), queries.dtype),
        in_specs=on_chip(REACH),
        out_specs=on_chip(1)[0],
        compiler_params=room(4),
        name="finish",
    )(*arrived)
    other = shifted(mine, "outer", 1)
    first = jnp.where(o == 0, mine, other)
    second = jnp.where(o == 0, other, mine)
    return jnp.concatenate([first, second], axis=0)


def solution(mesh):
    outer, inner, head = (mesh.shape[a] for a in ("outer", "inner", "head"))
    grid = Mesh(
        mesh.devices.reshape(outer, inner // COLUMNS, COLUMNS, head),
        ("outer", "z", "x", "head"),
    )
    tails = P(("z", "x"), "head", None)
    rows = P(("outer", "z", "x"), "head", None)
    return jax.shard_map(
        body, mesh=grid, in_specs=(tails, rows, rows, P()), out_specs=tails, check_vma=False
    )
```

```python
import functools
import math

import jax
import jax.numpy as jnp
from jax import lax
from jax.experimental import pallas as pl
from jax.experimental.pallas import tpu as pltpu
from jax.sharding import Mesh, PartitionSpec as P

BLOCK = 128
STEP = 512
NEGATIVE = -1e30
TAIL = 8
NOTHING = -32768.0
EXTRA = 8
CODED = 8
COLUMNS = 4
REACH = 4


def shifted(part, axes, by):
    size = lax.axis_size(axes)
    return lax.ppermute(part, axes, [(i, (i + by) % size) for i in range(size)])


def mask_kernel(blocks, lengths_ref, live_ref):
    rows, columns = lax.axis_size("z"), lax.axis_size("x")
    segment = (lax.axis_index("outer") * rows + lax.axis_index("z")) * columns + lax.axis_index("x")
    count = lengths_ref.shape[1]
    lengths = jnp.broadcast_to(lengths_ref[...].astype(jnp.float32), (count, count))
    upto = lax.broadcasted_iota(jnp.int32, (count, count), 0)
    which = lax.broadcasted_iota(jnp.int32, (count, count), 1)
    edges = jnp.sum(jnp.where(which <= upto, lengths, 0.0), axis=1, keepdims=True)
    here = (segment * blocks).astype(jnp.float32)
    last = here + (blocks - 1.0)
    start = jnp.max(jnp.where(edges <= last, edges, 0.0), axis=0, keepdims=True)
    end = jnp.min(jnp.where(edges > last, edges, 1e9), axis=0, keepdims=True)
    n_live = jnp.floor(end * (1.0 / blocks)) - segment.astype(jnp.float32)
    row = lax.broadcasted_iota(jnp.int32, live_ref.shape, 0)
    live_ref[...] = jnp.where(row == 0, n_live, start - here)


def own_kernel(kv_count, o_ref, q_ref, out_ref):
    tail = TAIL
    sharing = q_ref.shape[1] // kv_count
    mine = q_ref[pl.ds(o_ref[0] * tail, tail)].astype(jnp.float32)
    rows = [
        mine[:, h * sharing : (h + 1) * sharing, :].reshape(tail * sharing, -1)
        for h in range(kv_count)
    ]
    out_ref[...] = jnp.transpose(jnp.concatenate(rows, axis=0)).astype(out_ref.dtype)


def stack_kernel(*refs):
    blocks, out_ref = refs[:-1], refs[-1]
    kv_count = out_ref.shape[0]
    wide = out_ref.shape[2] // len(blocks)
    for h in range(kv_count):
        out_ref[h] = jnp.concatenate(
            [b[:, h * wide : (h + 1) * wide] for b in blocks], axis=1
        )


def write_exact(ref, o, m, l):
    dim = o.shape[0]
    row = lax.broadcasted_iota(jnp.int32, (EXTRA, o.shape[1]), 0)
    ref[:dim] = o
    ref[dim:] = jnp.where(row == 0, m, jnp.where(row == 1, l, 0.0))


def read_exact(ref, dim):
    return ref[:dim], ref[dim : dim + 1], ref[dim + 1 : dim + 2]


def write_coded(ref, o, m, l):
    dim = o.shape[0]
    most = jnp.maximum(jnp.max(jnp.abs(o), axis=0, keepdims=True), 1e-30)
    power = jnp.floor(jnp.log2(most) + 1e-3) + 1.0
    code = jnp.clip(jnp.floor(o * jnp.exp2(15.0 - power) + 0.5), -32767.0, 32767.0)
    high = jnp.floor(l * 2.0)
    low = jnp.floor((l * 2.0 - high) * 32768.0)
    row = lax.broadcasted_iota(jnp.int32, (CODED, o.shape[1]), 0)
    tail = jnp.where(row == 0, m, jnp.where(row == 1, high, jnp.where(row == 2, low, power)))
    ref[:dim] = code.astype(jnp.int32).astype(jnp.int16)
    ref[dim:] = tail.astype(jnp.int32).astype(jnp.int16)


def read_coded(ref, dim):
    tail = ref[dim:].astype(jnp.int32).astype(jnp.float32)
    m, high, low, power = (tail[k : k + 1] for k in range(4))
    o = ref[:dim].astype(jnp.int32).astype(jnp.float32) * jnp.exp2(power - 15.0)
    return o, m, (high + low * (1.0 / 32768.0)) * 0.5


def attend_kernel(own, factor, live_ref, q_ref, k_ref, v_ref, out_ref, s_ref):
    kv_count, key_rows, dim = k_ref.shape
    width = q_ref.shape[2]
    blocks = out_ref.shape[0]
    wide = width // blocks
    sharing = wide // TAIL
    lanes = kv_count * wide
    count = key_rows // BLOCK
    n_live, first = live_ref[0:1, 0:1], live_ref[1:2, 0:1]
    some = jnp.max(live_ref[0:1, :])
    write = write_exact if own == 0 else write_coded

    @pl.when(own >= some)
    def _():
        none = jnp.zeros((1, lanes), jnp.float32)
        for j in range(blocks):
            write(out_ref.at[j], jnp.zeros((dim, lanes), jnp.float32), none + NOTHING, none)

    def run(width, live_blocks):
        per = STEP // BLOCK
        steps = key_rows // STEP

        def score(h, c):
            s = jnp.dot(
                k_ref[h, c * STEP : (c + 1) * STEP, :], q_ref[h, :, :width], preferred_element_type=jnp.float32
            )
            s_ref[h, c * STEP : (c + 1) * STEP, :width] = s
            peak = jnp.full((8, width), NEGATIVE, jnp.float32)
            for b in range(per):
                rows = s[b * BLOCK : (b + 1) * BLOCK]
                if own == 0 and c * per + b == count - 1:
                    lane = lax.broadcasted_iota(jnp.int32, (8, width), 1)
                    late = lax.broadcasted_iota(jnp.int32, (8, width), 0)
                    ahead = (lane < wide) & (late > lane // sharing)
                    corner = jnp.where(ahead, NEGATIVE, rows[BLOCK - 8 :])
                    s_ref[h, key_rows - 8 :, :width] = corner
                    peak = jnp.maximum(peak, corner)
                    rows = rows[: BLOCK - 8]
                top = jnp.max(rows.reshape(-1, 8, width), axis=0)
                peak = jnp.maximum(peak, jnp.where(c * per + b >= first, top, NEGATIVE))
            return peak

        def weigh(h, c, top, total):
            parts = []
            for b in range(c * per, (c + 1) * per):
                s = s_ref[h, b * BLOCK : (b + 1) * BLOCK, :width]
                w = jnp.exp2((s - jnp.where(b >= first, top, -NEGATIVE)) * factor)
                total = total + jnp.sum(w.reshape(-1, 8, width), axis=0)
                parts.append(w.astype(jnp.bfloat16))
            return parts, total

        tops, totals, outputs = [], [], []
        peaks = [score(0, c) for c in range(steps)]
        for h in range(kv_count):
            tops.append(jnp.max(functools.reduce(jnp.maximum, peaks), axis=0, keepdims=True))
            peaks, parts, total = [], [], jnp.zeros((8, width), jnp.float32)
            for c in range(steps):
                more, total = weigh(h, c, tops[h], total)
                parts += more
                if h + 1 < kv_count:
                    peaks.append(score(h + 1, c))
            totals.append(jnp.sum(total, axis=0, keepdims=True))
            outputs.append(
                jnp.dot(v_ref[h], jnp.concatenate(parts, axis=0), preferred_element_type=jnp.float32)
            )
        none = jnp.zeros((1, lanes), jnp.float32)
        for j in range(live_blocks, blocks):
            write(out_ref.at[j], jnp.zeros((dim, lanes), jnp.float32), none + NOTHING, none)
        for j in range(live_blocks):
            here = slice(j * wide, (j + 1) * wide)
            keep = own + blocks * j < n_live
            o = jnp.concatenate([a[:, here] for a in outputs], axis=1)
            m = jnp.concatenate([a[:, here] for a in tops], axis=1) * factor
            l = jnp.concatenate([a[:, here] for a in totals], axis=1)
            whole = jnp.ceil(m)
            f = jnp.where(keep, jnp.exp2(m - whole), 0.0)
            write(
                out_ref.at[j], jnp.where(keep, o * f, 0.0), jnp.where(keep, whole, NOTHING), l * f
            )

    half = blocks // 2

    @pl.when((own < some) & (own + COLUMNS * half >= some))
    def _():
        run(half * wide, half)

    @pl.when(own + COLUMNS * half < some)
    def _():
        run(width, blocks)


def merge(parts):
    top = functools.reduce(jnp.maximum, [m for _, m, _ in parts])
    o = l = None
    for po, pm, pt in parts:
        f = jnp.exp2(pm - top)
        o = po * f if o is None else o + po * f
        l = pt * f if l is None else l + pt * f
    return o, top, l


def column_kernel(*refs):
    parts, outs = refs[:COLUMNS], refs[COLUMNS:]
    dim = outs[0].shape[0] - EXTRA
    for j, out in enumerate(outs):
        found = [read_exact(parts[0].at[j], dim)] + [read_coded(p.at[j], dim) for p in parts[1:]]
        write = write_exact if j == 0 else write_coded
        write(out, *merge(found))


def finish_kernel(kv_count, *refs):
    parts, out_ref = refs[:-1], refs[-1]
    dim = out_ref.shape[2]
    found = [read_exact(parts[0], dim)] + [read_coded(p, dim) for p in parts[1:]]
    o, _, l = merge(found)
    res = jnp.transpose(o / l).reshape(kv_count, TAIL, -1, dim)
    out_ref[...] = jnp.concatenate([res[h] for h in range(kv_count)], axis=1).astype(out_ref.dtype)


def on_chip(count):
    return [pl.BlockSpec(memory_space=pltpu.VMEM)] * count


def room(mebibytes):
    return pltpu.CompilerParams(vmem_limit_bytes=mebibytes << 20)


def scalars():
    return [pl.BlockSpec(memory_space=pltpu.SMEM)]


def body(queries, keys, values, doc_lengths):
    columns = lax.axis_size("x")
    o = lax.axis_index("outer")
    key_rows, kv_count, dim = keys.shape
    heads = queries.shape[1]
    sharing = heads // kv_count
    lanes = kv_count * TAIL * sharing
    width = REACH * TAIL * sharing
    factor = math.log2(math.e) / math.sqrt(dim)

    own = pl.pallas_call(
        functools.partial(own_kernel, kv_count),
        out_shape=jax.ShapeDtypeStruct((dim, lanes), queries.dtype),
        in_specs=scalars() + on_chip(1),
        out_specs=on_chip(1)[0],
        compiler_params=room(4),
        name="own_tails",
    )(o.reshape(1).astype(jnp.int32), queries)
    held = [own] + [shifted(own, ("outer", "z"), -j) for j in range(1, REACH)]

    live = pl.pallas_call(
        functools.partial(mask_kernel, key_rows // BLOCK),
        out_shape=jax.ShapeDtypeStruct((8, 128), jnp.float32),
        in_specs=on_chip(1),
        out_specs=on_chip(1)[0],
        compiler_params=room(4),
        name="mask",
    )(doc_lengths.reshape(1, -1))
    k_heads = jnp.transpose(keys, (1, 0, 2))
    v_heads = jnp.transpose(values, (1, 2, 0))
    held, live, k_heads, v_heads = lax.optimization_barrier((held, live, k_heads, v_heads))

    stack = pl.pallas_call(
        stack_kernel,
        out_shape=jax.ShapeDtypeStruct((kv_count, dim, width), queries.dtype),
        in_specs=on_chip(REACH),
        out_specs=on_chip(1)[0],
        compiler_params=room(4),
        name="stack_tails",
    )(*held)
    everywhere = ("outer", "z", "x")
    asked = [stack] + [shifted(stack, everywhere, -u) for u in range(1, columns)]

    exact = jax.ShapeDtypeStruct((REACH, dim + EXTRA, lanes), jnp.float32)
    coded = jax.ShapeDtypeStruct((REACH, dim + CODED, lanes), jnp.int16)
    partial = []
    for u in range(columns):
        block = asked[u]
        if u == 1:
            block, _ = lax.optimization_barrier((block, partial[0]))
        partial.append(
            pl.pallas_call(
                functools.partial(attend_kernel, u, factor),
                out_shape=exact if u == 0 else coded,
                in_specs=on_chip(4),
                out_specs=on_chip(1)[0],
                scratch_shapes=[pltpu.VMEM((kv_count, key_rows, width), jnp.float32)],
                cost_estimate=pl.CostEstimate(
                    flops=4 * kv_count * key_rows * width * dim,
                    bytes_accessed=4 * kv_count * key_rows * dim,
                    transcendentals=kv_count * key_rows * width,
                ),
                compiler_params=room(16),
                name=f"attend_{u}",
            )(live, block, k_heads, v_heads)
        )
    arrived = [partial[0]] + [shifted(partial[u], everywhere, u) for u in range(1, columns)]
    column = pl.pallas_call(
        column_kernel,
        out_shape=[jax.ShapeDtypeStruct((dim + EXTRA, lanes), jnp.float32)]
        + [jax.ShapeDtypeStruct((dim + CODED, lanes), jnp.int16)] * (REACH - 1),
        in_specs=on_chip(columns),
        out_specs=on_chip(REACH),
        compiler_params=room(4),
        name="merge_columns",
    )(*arrived)
    arrived = [column[0]] + [shifted(column[j], ("outer", "z"), j) for j in range(1, REACH)]
    mine = pl.pallas_call(
        functools.partial(finish_kernel, kv_count),
        out_shape=jax.ShapeDtypeStruct((TAIL, heads, dim), queries.dtype),
        in_specs=on_chip(REACH),
        out_specs=on_chip(1)[0],
        compiler_params=room(4),
        name="finish",
    )(*arrived)
    other = shifted(mine, "outer", 1)
    first = jnp.where(o == 0, mine, other)
    second = jnp.where(o == 0, other, mine)
    return jnp.concatenate([first, second], axis=0)


def solution(mesh):
    outer, inner, head = (mesh.shape[a] for a in ("outer", "inner", "head"))
    grid = Mesh(
        mesh.devices.reshape(outer, inner // COLUMNS, COLUMNS, head),
        ("outer", "z", "x", "head"),
    )
    tails = P(("z", "x"), "head", None)
    rows = P(("outer", "z", "x"), "head", None)
    return jax.shard_map(
        body, mesh=grid, in_specs=(tails, rows, rows, P()), out_specs=tails, check_vma=False
    )
```

```python
import functools
import math

import jax
import jax.numpy as jnp
from jax import lax
from jax.experimental import pallas as pl
from jax.experimental.pallas import tpu as pltpu
from jax.sharding import Mesh, PartitionSpec as P

BLOCK = 128
STEP = 512
NEGATIVE = -1e30
TAIL = 8
NOTHING = -32768.0
EXTRA = 8
CODED = 8
COLUMNS = 4
REACH = 4


def shifted(part, axes, by):
    size = lax.axis_size(axes)
    return lax.ppermute(part, axes, [(i, (i + by) % size) for i in range(size)])


def mask_kernel(blocks, lengths_ref, live_ref):
    rows, columns = lax.axis_size("z"), lax.axis_size("x")
    segment = (lax.axis_index("outer") * rows + lax.axis_index("z")) * columns + lax.axis_index("x")
    count = lengths_ref.shape[1]
    lengths = jnp.broadcast_to(lengths_ref[...].astype(jnp.float32), (count, count))
    upto = lax.broadcasted_iota(jnp.int32, (count, count), 0)
    which = lax.broadcasted_iota(jnp.int32, (count, count), 1)
    edges = jnp.sum(jnp.where(which <= upto, lengths, 0.0), axis=1, keepdims=True)
    here = (segment * blocks).astype(jnp.float32)
    last = here + (blocks - 1.0)
    start = jnp.max(jnp.where(edges <= last, edges, 0.0), axis=0, keepdims=True)
    end = jnp.min(jnp.where(edges > last, edges, 1e9), axis=0, keepdims=True)
    n_live = jnp.floor(end * (1.0 / blocks)) - segment.astype(jnp.float32)
    row = lax.broadcasted_iota(jnp.int32, live_ref.shape, 0)
    live_ref[...] = jnp.where(row == 0, n_live, start - here)


def stack_kernel(*refs):
    blocks, out_ref = refs[:-1], refs[-1]
    kv_count, dim, width = out_ref.shape
    tail, heads, _ = blocks[0].shape
    sharing = heads // kv_count
    whole = [b[...].astype(jnp.float32) for b in blocks]
    for h in range(kv_count):
        rows = [
            w[:, h * sharing : (h + 1) * sharing, :].reshape(tail * sharing, dim) for w in whole
        ]
        out_ref[h] = jnp.transpose(jnp.concatenate(rows, axis=0)).astype(out_ref.dtype)


def write_exact(ref, o, m, l):
    dim = o.shape[0]
    row = lax.broadcasted_iota(jnp.int32, (EXTRA, o.shape[1]), 0)
    ref[:dim] = o
    ref[dim:] = jnp.where(row == 0, m, jnp.where(row == 1, l, 0.0))


def read_exact(ref, dim):
    return ref[:dim], ref[dim : dim + 1], ref[dim + 1 : dim + 2]


def write_coded(ref, o, m, l):
    dim = o.shape[0]
    most = jnp.maximum(jnp.max(jnp.abs(o), axis=0, keepdims=True), 1e-30)
    power = jnp.floor(jnp.log2(most) + 1e-3) + 1.0
    code = jnp.clip(jnp.floor(o * jnp.exp2(15.0 - power) + 0.5), -32767.0, 32767.0)
    high = jnp.floor(l * 2.0)
    low = jnp.floor((l * 2.0 - high) * 32768.0)
    row = lax.broadcasted_iota(jnp.int32, (CODED, o.shape[1]), 0)
    tail = jnp.where(row == 0, m, jnp.where(row == 1, high, jnp.where(row == 2, low, power)))
    ref[:dim] = code.astype(jnp.int32).astype(jnp.int16)
    ref[dim:] = tail.astype(jnp.int32).astype(jnp.int16)


def read_coded(ref, dim):
    tail = ref[dim:].astype(jnp.int32).astype(jnp.float32)
    m, high, low, power = (tail[k : k + 1] for k in range(4))
    o = ref[:dim].astype(jnp.int32).astype(jnp.float32) * jnp.exp2(power - 15.0)
    return o, m, (high + low * (1.0 / 32768.0)) * 0.5


def attend_kernel(own, factor, live_ref, q_ref, k_ref, v_ref, out_ref, s_ref):
    kv_count, key_rows, dim = k_ref.shape
    width = q_ref.shape[2]
    blocks = out_ref.shape[0]
    wide = width // blocks
    sharing = wide // TAIL
    lanes = kv_count * wide
    count = key_rows // BLOCK
    n_live, first = live_ref[0:1, 0:1], live_ref[1:2, 0:1]
    some = jnp.max(live_ref[0:1, :])
    write = write_exact if own == 0 else write_coded

    @pl.when(own >= some)
    def _():
        none = jnp.zeros((1, lanes), jnp.float32)
        for j in range(blocks):
            write(out_ref.at[j], jnp.zeros((dim, lanes), jnp.float32), none + NOTHING, none)

    def run(width, live_blocks):
        per = STEP // BLOCK
        steps = key_rows // STEP

        def score(h, c):
            s = jnp.dot(
                k_ref[h, c * STEP : (c + 1) * STEP, :], q_ref[h, :, :width], preferred_element_type=jnp.float32
            )
            s_ref[h, c * STEP : (c + 1) * STEP, :width] = s
            peak = jnp.full((8, width), NEGATIVE, jnp.float32)
            for b in range(per):
                rows = s[b * BLOCK : (b + 1) * BLOCK]
                if own == 0 and c * per + b == count - 1:
                    lane = lax.broadcasted_iota(jnp.int32, (8, width), 1)
                    late = lax.broadcasted_iota(jnp.int32, (8, width), 0)
                    ahead = (lane < wide) & (late > lane // sharing)
                    corner = jnp.where(ahead, NEGATIVE, rows[BLOCK - 8 :])
                    s_ref[h, key_rows - 8 :, :width] = corner
                    peak = jnp.maximum(peak, corner)
                    rows = rows[: BLOCK - 8]
                top = jnp.max(rows.reshape(-1, 8, width), axis=0)
                peak = jnp.maximum(peak, jnp.where(c * per + b >= first, top, NEGATIVE))
            return peak

        def weigh(h, c, top, total):
            parts = []
            for b in range(c * per, (c + 1) * per):
                s = s_ref[h, b * BLOCK : (b + 1) * BLOCK, :width]
                w = jnp.exp2((s - jnp.where(b >= first, top, -NEGATIVE)) * factor)
                total = total + jnp.sum(w.reshape(-1, 8, width), axis=0)
                parts.append(w.astype(jnp.bfloat16))
            return parts, total

        tops, totals, outputs = [], [], []
        peaks = [score(0, c) for c in range(steps)]
        for h in range(kv_count):
            tops.append(jnp.max(functools.reduce(jnp.maximum, peaks), axis=0, keepdims=True))
            peaks, parts, total = [], [], jnp.zeros((8, width), jnp.float32)
            for c in range(steps):
                more, total = weigh(h, c, tops[h], total)
                parts += more
                if h + 1 < kv_count:
                    peaks.append(score(h + 1, c))
            totals.append(jnp.sum(total, axis=0, keepdims=True))
            outputs.append(
                jnp.dot(v_ref[h], jnp.concatenate(parts, axis=0), preferred_element_type=jnp.float32)
            )
        none = jnp.zeros((1, lanes), jnp.float32)
        for j in range(live_blocks, blocks):
            write(out_ref.at[j], jnp.zeros((dim, lanes), jnp.float32), none + NOTHING, none)
        for j in range(live_blocks):
            here = slice(j * wide, (j + 1) * wide)
            keep = own + blocks * j < n_live
            o = jnp.concatenate([a[:, here] for a in outputs], axis=1)
            m = jnp.concatenate([a[:, here] for a in tops], axis=1) * factor
            l = jnp.concatenate([a[:, here] for a in totals], axis=1)
            whole = jnp.ceil(m)
            f = jnp.where(keep, jnp.exp2(m - whole), 0.0)
            write(
                out_ref.at[j], jnp.where(keep, o * f, 0.0), jnp.where(keep, whole, NOTHING), l * f
            )

    half = blocks // 2

    @pl.when((own < some) & (own + COLUMNS * half >= some))
    def _():
        run(half * wide, half)

    @pl.when(own + COLUMNS * half < some)
    def _():
        run(width, blocks)


def merge(parts):
    top = functools.reduce(jnp.maximum, [m for _, m, _ in parts])
    o = l = None
    for po, pm, pt in parts:
        f = jnp.exp2(pm - top)
        o = po * f if o is None else o + po * f
        l = pt * f if l is None else l + pt * f
    return o, top, l


def column_kernel(*refs):
    parts, outs = refs[:COLUMNS], refs[COLUMNS:]
    dim = outs[0].shape[0] - EXTRA
    for j, out in enumerate(outs):
        found = [read_exact(parts[0].at[j], dim)] + [read_coded(p.at[j], dim) for p in parts[1:]]
        write = write_exact if j == 0 else write_coded
        write(out, *merge(found))


def finish_kernel(kv_count, *refs):
    parts, out_ref = refs[:-1], refs[-1]
    dim = out_ref.shape[2]
    found = [read_exact(parts[0], dim)] + [read_coded(p, dim) for p in parts[1:]]
    o, _, l = merge(found)
    res = jnp.transpose(o / l).reshape(kv_count, TAIL, -1, dim)
    out_ref[...] = jnp.concatenate([res[h] for h in range(kv_count)], axis=1).astype(out_ref.dtype)


def on_chip(count):
    return [pl.BlockSpec(memory_space=pltpu.VMEM)] * count


def room(mebibytes):
    return pltpu.CompilerParams(vmem_limit_bytes=mebibytes << 20)


def scalars():
    return [pl.BlockSpec(memory_space=pltpu.SMEM)]


def body(queries, keys, values, doc_lengths):
    columns = lax.axis_size("x")
    o = lax.axis_index("outer")
    key_rows, kv_count, dim = keys.shape
    heads = queries.shape[1]
    sharing = heads // kv_count
    lanes = kv_count * TAIL * sharing
    width = REACH * TAIL * sharing
    factor = math.log2(math.e) / math.sqrt(dim)

    own = lax.dynamic_slice_in_dim(queries, o * TAIL, TAIL, 0)
    held = [own] + [shifted(own, ("outer", "z"), -j) for j in range(1, REACH)]

    live = pl.pallas_call(
        functools.partial(mask_kernel, key_rows // BLOCK),
        out_shape=jax.ShapeDtypeStruct((8, 128), jnp.float32),
        in_specs=on_chip(1),
        out_specs=on_chip(1)[0],
        compiler_params=room(4),
        name="mask",
    )(doc_lengths.reshape(1, -1))
    k_heads = jnp.transpose(keys, (1, 0, 2))
    v_heads = jnp.transpose(values, (1, 2, 0))
    held, live, k_heads, v_heads = lax.optimization_barrier((held, live, k_heads, v_heads))

    stack = pl.pallas_call(
        stack_kernel,
        out_shape=jax.ShapeDtypeStruct((kv_count, dim, width), queries.dtype),
        in_specs=on_chip(REACH),
        out_specs=on_chip(1)[0],
        compiler_params=room(4),
        name="stack_tails",
    )(*held)
    everywhere = ("outer", "z", "x")
    asked = [stack] + [shifted(stack, everywhere, -u) for u in range(1, columns)]

    exact = jax.ShapeDtypeStruct((REACH, dim + EXTRA, lanes), jnp.float32)
    coded = jax.ShapeDtypeStruct((REACH, dim + CODED, lanes), jnp.int16)
    partial = []
    for u in range(columns):
        block = asked[u]
        if u == 1:
            block, _ = lax.optimization_barrier((block, partial[0]))
        partial.append(
            pl.pallas_call(
                functools.partial(attend_kernel, u, factor),
                out_shape=exact if u == 0 else coded,
                in_specs=on_chip(4),
                out_specs=on_chip(1)[0],
                scratch_shapes=[pltpu.VMEM((kv_count, key_rows, width), jnp.float32)],
                cost_estimate=pl.CostEstimate(
                    flops=4 * kv_count * key_rows * width * dim,
                    bytes_accessed=4 * kv_count * key_rows * dim,
                    transcendentals=kv_count * key_rows * width,
                ),
                compiler_params=room(16),
                name=f"attend_{u}",
            )(live, block, k_heads, v_heads)
        )
    arrived = [partial[0]] + [shifted(partial[u], everywhere, u) for u in range(1, columns)]
    column = pl.pallas_call(
        column_kernel,
        out_shape=[jax.ShapeDtypeStruct((dim + EXTRA, lanes), jnp.float32)]
        + [jax.ShapeDtypeStruct((dim + CODED, lanes), jnp.int16)] * (REACH - 1),
        in_specs=on_chip(columns),
        out_specs=on_chip(REACH),
        compiler_params=room(4),
        name="merge_columns",
    )(*arrived)
    arrived = [column[0]] + [shifted(column[j], ("outer", "z"), j) for j in range(1, REACH)]
    mine = pl.pallas_call(
        functools.partial(finish_kernel, kv_count),
        out_shape=jax.ShapeDtypeStruct((TAIL, heads, dim), queries.dtype),
        in_specs=on_chip(REACH),
        out_specs=on_chip(1)[0],
        compiler_params=room(4),
        name="finish",
    )(*arrived)
    other = shifted(mine, "outer", 1)
    first = jnp.where(o == 0, mine, other)
    second = jnp.where(o == 0, other, mine)
    return jnp.concatenate([first, second], axis=0)


def solution(mesh):
    outer, inner, head = (mesh.shape[a] for a in ("outer", "inner", "head"))
    grid = Mesh(
        mesh.devices.reshape(outer, inner // COLUMNS, COLUMNS, head),
        ("outer", "z", "x", "head"),
    )
    tails = P(("z", "x"), "head", None)
    rows = P(("outer", "z", "x"), "head", None)
    return jax.shard_map(
        body, mesh=grid, in_specs=(tails, rows, rows, P()), out_specs=tails, check_vma=False
    )
```

```python
import functools
import math

import jax
import jax.numpy as jnp
from jax import lax
from jax.experimental import pallas as pl
from jax.experimental.pallas import tpu as pltpu
from jax.sharding import Mesh, PartitionSpec as P

BLOCK = 128
STEP = 512
NEGATIVE = -1e30
TAIL = 8
NOTHING = -32768.0
EXTRA = 8
CODED = 8
COLUMNS = 4
REACH = 4


def shifted(part, axes, by):
    size = lax.axis_size(axes)
    return lax.ppermute(part, axes, [(i, (i + by) % size) for i in range(size)])


def mask_kernel(blocks, lengths_ref, live_ref):
    rows, columns = lax.axis_size("z"), lax.axis_size("x")
    segment = (lax.axis_index("outer") * rows + lax.axis_index("z")) * columns + lax.axis_index("x")
    count = lengths_ref.shape[1]
    lengths = jnp.broadcast_to(lengths_ref[...].astype(jnp.float32), (count, count))
    upto = lax.broadcasted_iota(jnp.int32, (count, count), 0)
    which = lax.broadcasted_iota(jnp.int32, (count, count), 1)
    edges = jnp.sum(jnp.where(which <= upto, lengths, 0.0), axis=1, keepdims=True)
    here = (segment * blocks).astype(jnp.float32)
    last = here + (blocks - 1.0)
    start = jnp.max(jnp.where(edges <= last, edges, 0.0), axis=0, keepdims=True)
    end = jnp.min(jnp.where(edges > last, edges, 1e9), axis=0, keepdims=True)
    n_live = jnp.floor(end * (1.0 / blocks)) - segment.astype(jnp.float32)
    row = lax.broadcasted_iota(jnp.int32, live_ref.shape, 0)
    live_ref[...] = jnp.where(row == 0, n_live, start - here)


def stack_kernel(*refs):
    blocks, out_ref = refs[:-1], refs[-1]
    kv_count, dim, width = out_ref.shape
    tail, heads, _ = blocks[0].shape
    sharing = heads // kv_count
    whole = [b[...].astype(jnp.float32) for b in blocks]
    for h in range(kv_count):
        rows = [
            w[:, h * sharing : (h + 1) * sharing, :].reshape(tail * sharing, dim) for w in whole
        ]
        out_ref[h] = jnp.transpose(jnp.concatenate(rows, axis=0)).astype(out_ref.dtype)


def write_exact(ref, o, m, l):
    dim = o.shape[0]
    row = lax.broadcasted_iota(jnp.int32, (EXTRA, o.shape[1]), 0)
    ref[:dim] = o
    ref[dim:] = jnp.where(row == 0, m, jnp.where(row == 1, l, 0.0))


def read_exact(ref, dim):
    return ref[:dim], ref[dim : dim + 1], ref[dim + 1 : dim + 2]


def write_coded(ref, o, m, l):
    dim = o.shape[0]
    most = jnp.maximum(jnp.max(jnp.abs(o), axis=0, keepdims=True), 1e-30)
    power = jnp.floor(jnp.log2(most) + 1e-3) + 1.0
    code = jnp.clip(jnp.floor(o * jnp.exp2(15.0 - power) + 0.5), -32767.0, 32767.0)
    high = jnp.floor(l * 2.0)
    low = jnp.floor((l * 2.0 - high) * 32768.0)
    row = lax.broadcasted_iota(jnp.int32, (CODED, o.shape[1]), 0)
    tail = jnp.where(row == 0, m, jnp.where(row == 1, high, jnp.where(row == 2, low, power)))
    ref[:dim] = code.astype(jnp.int32).astype(jnp.int16)
    ref[dim:] = tail.astype(jnp.int32).astype(jnp.int16)


def read_coded(ref, dim):
    tail = ref[dim:].astype(jnp.int32).astype(jnp.float32)
    m, high, low, power = (tail[k : k + 1] for k in range(4))
    o = ref[:dim].astype(jnp.int32).astype(jnp.float32) * jnp.exp2(power - 15.0)
    return o, m, (high + low * (1.0 / 32768.0)) * 0.5


def attend_kernel(own, factor, live_ref, q_ref, k_ref, v_ref, out_ref, s_ref):
    kv_count, key_rows, dim = k_ref.shape
    width = q_ref.shape[2]
    blocks = out_ref.shape[0]
    wide = width // blocks
    sharing = wide // TAIL
    lanes = kv_count * wide
    count = key_rows // BLOCK
    n_live, first = live_ref[0:1, 0:1], live_ref[1:2, 0:1]
    some = jnp.max(live_ref[0:1, :])
    write = write_exact if own == 0 else write_coded

    @pl.when(own >= some)
    def _():
        none = jnp.zeros((1, lanes), jnp.float32)
        for j in range(blocks):
            write(out_ref.at[j], jnp.zeros((dim, lanes), jnp.float32), none + NOTHING, none)

    def run(width, live_blocks):
        per = STEP // BLOCK
        steps = key_rows // STEP

        def score(h, c):
            s = jnp.dot(
                k_ref[h, c * STEP : (c + 1) * STEP, :], q_ref[h, :, :width], preferred_element_type=jnp.float32
            )
            s_ref[h, c * STEP : (c + 1) * STEP, :width] = s
            peak = jnp.full((8, width), NEGATIVE, jnp.float32)
            for b in range(per):
                rows = s[b * BLOCK : (b + 1) * BLOCK]
                if own == 0 and c * per + b == count - 1:
                    lane = lax.broadcasted_iota(jnp.int32, (8, width), 1)
                    late = lax.broadcasted_iota(jnp.int32, (8, width), 0)
                    ahead = (lane < wide) & (late > lane // sharing)
                    corner = jnp.where(ahead, NEGATIVE, rows[BLOCK - 8 :])
                    s_ref[h, key_rows - 8 :, :width] = corner
                    peak = jnp.maximum(peak, corner)
                    rows = rows[: BLOCK - 8]
                top = jnp.max(rows.reshape(-1, 8, width), axis=0)
                peak = jnp.maximum(peak, jnp.where(c * per + b >= first, top, NEGATIVE))
            return peak

        def weigh(h, c, top, total):
            parts = []
            for b in range(c * per, (c + 1) * per):
                s = s_ref[h, b * BLOCK : (b + 1) * BLOCK, :width]
                w = jnp.exp2((s - jnp.where(b >= first, top, -NEGATIVE)) * factor)
                total = total + jnp.sum(w.reshape(-1, 8, width), axis=0)
                parts.append(w.astype(jnp.bfloat16))
            return parts, total

        tops, totals, outputs = [], [], []
        peaks = [score(0, c) for c in range(steps)]
        for h in range(kv_count):
            tops.append(jnp.max(functools.reduce(jnp.maximum, peaks), axis=0, keepdims=True))
            peaks, parts, total = [], [], jnp.zeros((8, width), jnp.float32)
            for c in range(steps):
                more, total = weigh(h, c, tops[h], total)
                parts += more
                if h + 1 < kv_count:
                    peaks.append(score(h + 1, c))
            totals.append(jnp.sum(total, axis=0, keepdims=True))
            outputs.append(
                jnp.dot(v_ref[h], jnp.concatenate(parts, axis=0), preferred_element_type=jnp.float32)
            )
        none = jnp.zeros((1, lanes), jnp.float32)
        for j in range(live_blocks, blocks):
            write(out_ref.at[j], jnp.zeros((dim, lanes), jnp.float32), none + NOTHING, none)
        for j in range(live_blocks):
            here = slice(j * wide, (j + 1) * wide)
            keep = own + blocks * j < n_live
            o = jnp.concatenate([a[:, here] for a in outputs], axis=1)
            m = jnp.concatenate([a[:, here] for a in tops], axis=1) * factor
            l = jnp.concatenate([a[:, here] for a in totals], axis=1)
            whole = jnp.ceil(m)
            f = jnp.where(keep, jnp.exp2(m - whole), 0.0)
            write(
                out_ref.at[j], jnp.where(keep, o * f, 0.0), jnp.where(keep, whole, NOTHING), l * f
            )

    half = blocks // 2

    @pl.when((own < some) & (own + COLUMNS * half >= some))
    def _():
        run(half * wide, half)

    @pl.when(own + COLUMNS * half < some)
    def _():
        run(width, blocks)


def merge(parts):
    top = functools.reduce(jnp.maximum, [m for _, m, _ in parts])
    o = l = None
    for po, pm, pt in parts:
        f = jnp.exp2(pm - top)
        o = po * f if o is None else o + po * f
        l = pt * f if l is None else l + pt * f
    return o, top, l


def column_kernel(*refs):
    parts, outs = refs[:COLUMNS], refs[COLUMNS:]
    dim = outs[0].shape[0] - EXTRA
    for j, out in enumerate(outs):
        found = [read_exact(parts[0].at[j], dim)] + [read_coded(p.at[j], dim) for p in parts[1:]]
        write = write_exact if j == 0 else write_coded
        write(out, *merge(found))


def finish_kernel(kv_count, *refs):
    parts, out_ref = refs[:-1], refs[-1]
    dim = out_ref.shape[2]
    found = [read_exact(parts[0], dim)] + [read_coded(p, dim) for p in parts[1:]]
    o, _, l = merge(found)
    res = jnp.transpose(o / l).reshape(kv_count, TAIL, -1, dim)
    out_ref[...] = jnp.concatenate([res[h] for h in range(kv_count)], axis=1).astype(out_ref.dtype)


def place_kernel(mine_ref, other_ref, out_ref, sems):
    core = lax.axis_index("outer")
    tail = mine_ref.shape[0]
    own = pltpu.make_async_copy(mine_ref, out_ref.at[pl.ds(core * tail, tail)], sems.at[0])
    far = pltpu.make_async_copy(other_ref, out_ref.at[pl.ds((1 - core) * tail, tail)], sems.at[1])
    own.start()
    far.start()
    own.wait()
    far.wait()


def on_chip(count):
    return [pl.BlockSpec(memory_space=pltpu.VMEM)] * count


def room(mebibytes):
    return pltpu.CompilerParams(vmem_limit_bytes=mebibytes << 20)


def scalars():
    return [pl.BlockSpec(memory_space=pltpu.SMEM)]


def body(queries, keys, values, doc_lengths):
    columns = lax.axis_size("x")
    o = lax.axis_index("outer")
    key_rows, kv_count, dim = keys.shape
    heads = queries.shape[1]
    sharing = heads // kv_count
    lanes = kv_count * TAIL * sharing
    width = REACH * TAIL * sharing
    factor = math.log2(math.e) / math.sqrt(dim)

    own = lax.dynamic_slice_in_dim(queries, o * TAIL, TAIL, 0)
    held = [own] + [shifted(own, ("outer", "z"), -j) for j in range(1, REACH)]

    live = pl.pallas_call(
        functools.partial(mask_kernel, key_rows // BLOCK),
        out_shape=jax.ShapeDtypeStruct((8, 128), jnp.float32),
        in_specs=on_chip(1),
        out_specs=on_chip(1)[0],
        compiler_params=room(4),
        name="mask",
    )(doc_lengths.reshape(1, -1))
    k_heads = jnp.transpose(keys, (1, 0, 2))
    v_heads = jnp.transpose(values, (1, 2, 0))
    held, live, k_heads, v_heads = lax.optimization_barrier((held, live, k_heads, v_heads))

    stack = pl.pallas_call(
        stack_kernel,
        out_shape=jax.ShapeDtypeStruct((kv_count, dim, width), queries.dtype),
        in_specs=on_chip(REACH),
        out_specs=on_chip(1)[0],
        compiler_params=room(4),
        name="stack_tails",
    )(*held)
    everywhere = ("outer", "z", "x")
    asked = [stack] + [shifted(stack, everywhere, -u) for u in range(1, columns)]

    exact = jax.ShapeDtypeStruct((REACH, dim + EXTRA, lanes), jnp.float32)
    coded = jax.ShapeDtypeStruct((REACH, dim + CODED, lanes), jnp.int16)
    partial = []
    for u in range(columns):
        block = asked[u]
        if u == 1:
            block, _ = lax.optimization_barrier((block, partial[0]))
        partial.append(
            pl.pallas_call(
                functools.partial(attend_kernel, u, factor),
                out_shape=exact if u == 0 else coded,
                in_specs=on_chip(4),
                out_specs=on_chip(1)[0],
                scratch_shapes=[pltpu.VMEM((kv_count, key_rows, width), jnp.float32)],
                cost_estimate=pl.CostEstimate(
                    flops=4 * kv_count * key_rows * width * dim,
                    bytes_accessed=4 * kv_count * key_rows * dim,
                    transcendentals=kv_count * key_rows * width,
                ),
                compiler_params=room(16),
                name=f"attend_{u}",
            )(live, block, k_heads, v_heads)
        )
    arrived = [partial[0]] + [shifted(partial[u], everywhere, u) for u in range(1, columns)]
    column = pl.pallas_call(
        column_kernel,
        out_shape=[jax.ShapeDtypeStruct((dim + EXTRA, lanes), jnp.float32)]
        + [jax.ShapeDtypeStruct((dim + CODED, lanes), jnp.int16)] * (REACH - 1),
        in_specs=on_chip(columns),
        out_specs=on_chip(REACH),
        compiler_params=room(4),
        name="merge_columns",
    )(*arrived)
    arrived = [column[0]] + [shifted(column[j], ("outer", "z"), j) for j in range(1, REACH)]
    mine = pl.pallas_call(
        functools.partial(finish_kernel, kv_count),
        out_shape=jax.ShapeDtypeStruct((TAIL, heads, dim), queries.dtype),
        in_specs=on_chip(REACH),
        out_specs=on_chip(1)[0],
        compiler_params=room(4),
        name="finish",
    )(*arrived)
    other = shifted(mine, "outer", 1)
    return pl.pallas_call(
        place_kernel,
        out_shape=jax.ShapeDtypeStruct(queries.shape, queries.dtype),
        in_specs=on_chip(2),
        out_specs=pl.BlockSpec(memory_space=pltpu.HBM),
        scratch_shapes=[pltpu.SemaphoreType.DMA((2,))],
        compiler_params=room(4),
        name="place",
    )(mine, other)


def solution(mesh):
    outer, inner, head = (mesh.shape[a] for a in ("outer", "inner", "head"))
    grid = Mesh(
        mesh.devices.reshape(outer, inner // COLUMNS, COLUMNS, head),
        ("outer", "z", "x", "head"),
    )
    tails = P(("z", "x"), "head", None)
    rows = P(("outer", "z", "x"), "head", None)
    return jax.shard_map(
        body, mesh=grid, in_specs=(tails, rows, rows, P()), out_specs=tails, check_vma=False
    )
```
